32 devices in a mesh: grp: 2 (over y), feat: 4 (over z), samp: 4 (over x, core).
Axes of the slice: x: 2, y: 2, z: 4, core: 2. Of those that a mesh axis runs over, the one named last changes fastest.
Arguments:
- embeddings: bfloat16 [8192, 1024], P(('grp', 'samp')), parts along dimension 0, may hold values from -6 to 6
- sign_bits: int32 [4096], P('feat'), may hold values 0 or 1
- perms: int32 [4, 1024], P('feat'), may hold values from 0 to 1023, each once within a row
- gauss: float32 [4096], P('feat'), may hold values from -4 to 4
- scale: float32 [4096], P('feat'), may hold values from 0.5 to 2
- phase: float32 [4096], P('feat'), may hold values from -3.140625 to 3.140625
- basis: float32 [128, 4096], P('grp', 'feat'), parts along dimension 0, may hold values from -40 to 40
Outputs:
- basis_out: float32 [128, 4096], P('grp', 'feat'), parts along dimension 0
- projections: float32 [128, 4096], P('grp', 'samp'), parts along dimension 0
The draws below stay inside these ranges and needn't reach their ends.
There are 2 independent parts, one for each index of `grp`. The reference program is written for one: setup_inputs(seed, part) draws one part's arguments, and reference() takes and returns one part's arrays. A program takes and returns all parts, laid end to end along the dimension named above; an argument that names none is the same for every part. Nothing has to cross between parts.
Inputs may be any that keep to these rules, and one draw needn't show every extreme that they name: Each row of perms names every number of 0 to 1023 once.
All inputs are finite; a program needn't handle non-finite values. No bound on the sum of `sign_bits` on one device may be relied on, other than what follows from the above.
Results may differ from the reference program's by a relative error of at most 0.0057.
Values sent between devices are 32-bit elements; how exact they have to be, the bound alone decides.
A program may use at most 64 MiB of HBM per device.

```python
import math
import jax
import jax.numpy as jnp
from jax import lax

D = 1024
K = 64
BLOCKS = 4
FEATURES = 4096
SPAN = 4096


def draw_basis(key, part):
    base = jax.random.normal(jax.random.fold_in(key, 11), (K, FEATURES), jnp.float32)
    where = jnp.arange(FEATURES, dtype=jnp.float32)[None, :] / (FEATURES - 1)
    rising = jnp.exp(math.log(6.0) * where)
    return jnp.clip(base, -6.0, 6.0) * rising


def touch_ends(drawn, key, low, top_value):
    longest = drawn.shape.index(max(drawn.shape))
    spots = []
    for shift in (0, 1):
        where = [jax.random.randint(jax.random.fold_in(key, axis), (), 0, length) for axis, length in enumerate(drawn.shape)]
        where[longest] = (where[longest] + shift) % drawn.shape[longest]
        spots.append(tuple(where))
    return drawn.at[spots[0]].set(low).at[spots[1]].set(top_value)


def shard_levels(own_key, dims, shards, smallest, largest):
    def one(axis_at, shards_of):
        steps = jax.random.uniform(jax.random.fold_in(jax.random.fold_in(own_key, 6), axis_at), (shards_of,), jnp.float32, smallest / len(shards), largest / len(shards))
        return jnp.repeat(jnp.exp(steps), dims[axis_at] // shards_of).reshape((-1,) + (1,) * (len(dims) - axis_at - 1))

    loudness = one(*shards[0])
    for cut in shards[1:]:
        loudness = loudness * one(*cut)
    return loudness


def scatter_about(rng, dims, scale, limit, split=(), kind=jnp.bfloat16):
    values = jax.random.normal(rng, dims, jnp.float32) * scale
    if len(split) > 0:
        values = shard_levels(rng, dims, split, -0.22, 0.18) * values
    return jnp.clip(values, min=-limit, max=limit).astype(kind)


def setup_inputs(seed: int = 0, part: int = 0) -> dict:
    key_list = jax.random.split(jax.random.key(seed), 8)
    own_keys = jax.random.split(jax.random.fold_in(key_list[7], part), 8)
    return {
        "embeddings": scatter_about(own_keys[0], (SPAN, D), 1.0, 6.0, ((0, 4),)),
        "sign_bits": touch_ends((jax.random.randint(key_list[1], (FEATURES,), 0, 2) < 1).astype(jnp.int32), jax.random.fold_in(key_list[1], 1), 0, 1),
        "perms": jax.vmap(lambda own: jax.random.permutation(own, D))(jax.random.split(key_list[2], BLOCKS)).reshape((BLOCKS, D)).astype(jnp.int32),
        "gauss": scatter_about(key_list[3], (FEATURES,), 1.0, 4.0, ((0, 4),), jnp.float32),
        "scale": jnp.clip(jnp.exp(math.log(2.0) - 1.3862944 * jax.random.uniform(key_list[4], (FEATURES,), jnp.float32) ** shard_levels(key_list[4], (FEATURES,), ((0, 4),), -0.2, 0.2)), 0.5, 2.0),
        "phase": jnp.clip(jax.random.uniform(key_list[5], (FEATURES,), jnp.float32, -3.140625, 3.140625), -3.140625, 3.140625),
        "basis": draw_basis(jax.random.fold_in(jax.random.fold_in(key_list[7], part), 71), part),
    }


def walsh(values):
    width = values.shape[-1]
    leading = values.shape[:-1]
    stride = 1
    while stride < width:
        folded = values.reshape(leading + (width // (2 * stride), 2, stride))
        upper = folded[..., 0, :]
        lower = folded[..., 1, :]
        values = jnp.stack([upper + lower, upper - lower], axis=-2).reshape(leading + (width,))
        stride = stride * 2
    return values

def block_features(embeddings, bits, order, gauss, scale, phase):
    signs = (2 * bits - 1).astype(jnp.bfloat16)
    first = walsh((embeddings * signs).astype(jnp.float32)).astype(jnp.bfloat16)
    picked = jnp.take(first, order, axis=1)
    mixed = (picked.astype(jnp.float32) * gauss).astype(jnp.bfloat16)
    freq = walsh(mixed.astype(jnp.float32)) * scale / D + phase
    return (math.sqrt(2.0) * jnp.cos(freq)).astype(jnp.bfloat16)

def features_of(block, embeddings, sign_bits, perms, gauss, scale, phase):
    start = (block * D).astype(jnp.int32)
    return block_features(embeddings, lax.dynamic_slice_in_dim(sign_bits, start, D), perms[block], lax.dynamic_slice_in_dim(gauss, start, D), lax.dynamic_slice_in_dim(scale, start, D), lax.dynamic_slice_in_dim(phase, start, D))

def orthonormal(grown):
    gram = jnp.dot(grown, grown.T, precision=lax.Precision.HIGHEST) / FEATURES
    lower = jnp.linalg.cholesky(gram)
    return jax.scipy.linalg.solve_triangular(lower, grown, lower=True)

def reference(embeddings, sign_bits, perms, gauss, scale, phase, basis):
    basis_low = basis.astype(jnp.bfloat16)
    blocks = jnp.arange(BLOCKS, dtype=jnp.int32)

    def score_step(total, block):
        feats = features_of(block, embeddings, sign_bits, perms, gauss, scale, phase)
        piece = lax.dynamic_slice_in_dim(basis_low, (block * D).astype(jnp.int32), D, 1)
        return (total + jnp.dot(piece.astype(jnp.float32), feats.T.astype(jnp.float32), preferred_element_type=jnp.float32), None)
    total, _ = lax.scan(score_step, jnp.zeros((K, SPAN), jnp.float32), blocks)
    projections = total / math.sqrt(FEATURES)
    proj_low = projections.astype(jnp.bfloat16)

    def update_block(block):
        feats = features_of(block, embeddings, sign_bits, perms, gauss, scale, phase)
        return jnp.dot(proj_low.astype(jnp.float32), feats.astype(jnp.float32), preferred_element_type=jnp.float32)
    update = lax.map(update_block, blocks)
    update = jnp.transpose(update, (1, 0, 2)).reshape(K, FEATURES)
    grown = basis + update / math.sqrt(SPAN)
    basis_out = orthonormal(grown)
    return (basis_out, projections)
```

```python
import functools
import math

import jax
import jax.numpy as jnp
import numpy as np
from jax import lax
from jax.experimental import pallas as pl
from jax.experimental.pallas import tpu as pltpu
from jax.sharding import PartitionSpec as P

MESH = pl.DeviceIdType.MESH
BLOCK = 256
HIGHEST = lax.Precision.HIGHEST


def cosine_coefficients(degree):
    nodes = np.cos(np.pi * (np.arange(400) + 0.5) / 400)
    squares = (nodes + 1) / 8
    fitted = np.polynomial.Chebyshev.fit(
        squares, np.cos(2 * np.pi * np.sqrt(squares)), degree, domain=[0, 0.25]
    )
    return [float(c) * math.sqrt(2.0) for c in fitted.convert(kind=np.polynomial.Polynomial).coef]


COS = cosine_coefficients(6)


def parity_sign(bits):
    for shift in (8, 4, 2, 1):
        bits = bits ^ jnp.right_shift(bits, shift)
    return (1 - 2 * (bits & 1)).astype(jnp.float32)


def scaled_cosine(turns):
    rest = turns - jnp.round(turns)
    square = rest * rest
    total = jnp.full_like(square, COS[-1])
    for c in COS[-2::-1]:
        total = total * square + c
    return total


def transform(blocks):
    stride = 1
    while stride < len(blocks):
        result = list(blocks)
        for i in range(len(blocks)):
            if not i & stride:
                result[i] = blocks[i] + blocks[i + stride]
                result[i + stride] = blocks[i] - blocks[i + stride]
        blocks = result
        stride *= 2
    return blocks


def split(x):
    high = x.astype(jnp.bfloat16)
    rest = x - high.astype(jnp.float32)
    middle = rest.astype(jnp.bfloat16)
    low = (rest - middle.astype(jnp.float32)).astype(jnp.bfloat16)
    return high, middle, low


def inverse_factor(gram):
    size = gram.shape[0]
    row = lax.broadcasted_iota(jnp.int32, (8, size), 0)
    lane = lax.broadcasted_iota(jnp.int32, (8, size), 1)
    width = 2 * size
    sub = lax.broadcasted_iota(jnp.int32, (8, width), 0)
    groups = [
        jnp.concatenate(
            [(lane == row + 8 * g).astype(jnp.float32), gram[8 * g : 8 * g + 8]], axis=1
        )
        for g in range(size // 8)
    ]
    pivots = [jnp.ones((8, width), jnp.float32) for _ in groups]
    step = 8

    def spread(x):
        return jnp.broadcast_to(x, (8, width))

    for own in range(size // 8):
        first = size + own * step
        live = range(own, size // 8)
        rows = [spread(groups[own][k : k + 1]) for k in range(step)]
        cols = [
            {g: spread(groups[g][:, first + k : first + k + 1]) for g in live}
            for k in range(step)
        ]
        cross = {
            (k, m): spread(cols[m][own][k : k + 1]) for k in range(step) for m in range(k + 1)
        }
        for k in range(step):
            inverse = 1.0 / cross[k, k]
            pivots[own] = jnp.where(sub == k, cross[k, k], pivots[own])
            factor = {later: cross[later, k] * inverse for later in range(k + 1, step)}
            for later in range(k + 1, step):
                for m in range(k + 1, later + 1):
                    cross[later, m] = cross[later, m] - factor[later] * cross[m, k]
            for later in range(k + 1, step):
                rows[later] = rows[later] - factor[later] * rows[k]
                for g in live:
                    cols[later][g] = cols[later][g] - factor[later] * cols[k][g]
            for g in live:
                weight = cols[k][g] * inverse
                if g == own:
                    weight = jnp.where(sub > k, weight, 0.0)
                groups[g] = groups[g] - weight * rows[k]
    scaled = [g / jnp.sqrt(p) for g, p in zip(groups, pivots)]
    return jnp.concatenate(scaled, axis=0)[:, :size]


def kernel(
    feats, samps, emb_in, bits_in, perm_in, gauss_in, scale_in, phase_in, basis_in,
    proj, grown, gram_out,
    emb, bits, perm, gauss, scale, phase, basis,
    table, small, features, even, odd, scores, score_recv,
    upd, upd_recv, pair, halves, grams,
    s1, r1, s2, r2, s3, r3, s4, r4, s5, r5, loads, emb_loads,
):
    me = lax.axis_index("feat")
    my = lax.axis_index("samp")
    rows, width = emb.shape
    order = basis.shape[1]
    pieces = rows // BLOCK
    share = order // feats
    half = width // 2
    core = lax.rem(my, 2)
    sibling = my + 1 - 2 * core
    partner = lax.rem(my + 2, samps)
    blocks = width // BLOCK

    def piece_rows(i):
        return slice(i * BLOCK, (i + 1) * BLOCK)

    def share_rows(owner):
        return pl.ds(pl.multiple_of(owner * share, share), share)

    def half_cols(which):
        return slice(which * half, (which + 1) * half)

    emb_copies = [
        pltpu.make_async_copy(
            emb_in.at[piece_rows(i), :], emb.at[piece_rows(i), :], emb_loads.at[i]
        )
        for i in range(pieces)
    ]
    pairs = (
        (perm_in, perm), (bits_in, bits), (gauss_in, gauss), (scale_in, scale),
        (phase_in, phase), (basis_in.at[:, half_cols(0)], basis.at[0]),
        (basis_in.at[:, half_cols(1)], basis.at[1]),
    )
    parameters = [
        pltpu.make_async_copy(source, place, loads.at[n])
        for n, (source, place) in enumerate(pairs)
    ]
    for load in parameters[:-2]:
        load.start()
    emb_copies[0].start()
    for load in parameters[-2:]:
        load.start()
    for load in emb_copies[1:]:
        load.start()
    barrier = pltpu.get_barrier_semaphore()
    others = [lax.rem(me + d, feats) for d in range(1, feats)]
    for to in others:
        pl.semaphore_signal(barrier, inc=1, device_id={"feat": to}, device_id_type=MESH)
    for to in (sibling, partner):
        pl.semaphore_signal(barrier, inc=1, device_id={"samp": to}, device_id_type=MESH)

    square = (BLOCK, BLOCK)
    small[...] = parity_sign(
        lax.broadcasted_iota(jnp.int32, square, 0) & lax.broadcasted_iota(jnp.int32, square, 1)
    ).astype(jnp.bfloat16)
    parameters[0].wait()
    places = perm[...]
    base = parity_sign(lax.broadcasted_iota(jnp.int32, (128, width), 0) & places & 127).astype(
        jnp.bfloat16
    )
    for a in range(width // 128):
        flips = parity_sign(jnp.right_shift(places, 7) & a).astype(jnp.bfloat16)
        table[a * 128 : (a + 1) * 128, :] = base * flips
    for load in parameters[1:]:
        load.wait()
    signs = (2 * bits[...] - 1).astype(jnp.float32).astype(jnp.bfloat16)
    gains = gauss[...]
    rate = scale[...] * (1.0 / (2.0 * math.pi * width))
    offset = phase[...] * (1.0 / (2.0 * math.pi))
    basis_low = jnp.concatenate([basis[0], basis[1]], axis=1).astype(jnp.bfloat16)

    def copy(src, dst, send, recv, axis, to):
        return pltpu.make_async_remote_copy(
            src_ref=src, dst_ref=dst, send_sem=send, recv_sem=recv,
            device_id={axis: to}, device_id_type=MESH,
        )

    mixes = (even, odd)

    def mix(i, n):
        cols = slice(n * BLOCK, (n + 1) * BLOCK)
        signed = emb[piece_rows(i), :] * signs
        first = jnp.dot(signed, table[:, cols], preferred_element_type=jnp.float32)
        first = first.astype(jnp.bfloat16).astype(jnp.float32)
        mixes[i % 2][:, cols] = (first * gains[:, cols]).astype(jnp.bfloat16)

    def second(i):
        mixed = mixes[i % 2]
        return transform([
            jnp.dot(
                mixed[:, n * BLOCK : (n + 1) * BLOCK], small[...],
                preferred_element_type=jnp.float32,
            )
            for n in range(blocks)
        ])

    def wave(i, n, part):
        cols = slice(n * BLOCK, (n + 1) * BLOCK)
        turns = part * rate[:, cols] + offset[:, cols]
        features[piece_rows(i), cols] = scaled_cosine(turns).astype(jnp.bfloat16)

    def score(i):
        scores[i] = lax.dot_general(
            basis_low, features[piece_rows(i), :], (((1,), (1,)), ((), ())),
            preferred_element_type=jnp.float32,
        )

    def score_copy(i, owner, source, to):
        return copy(
            scores.at[i, share_rows(owner), :], score_recv.at[i, source],
            s1.at[i, to], r1.at[i, source], "feat", to,
        )

    def send_scores(i):
        for to in others:
            score_copy(i, to, me, to).start()

    emb_copies[0].wait()
    for n in range(blocks):
        mix(0, n)
    for i in range(pieces):
        if i + 1 < pieces:
            emb_copies[i + 1].wait()
        parts = second(i)
        for n in range(blocks):
            if i + 1 < pieces:
                mix(i + 1, n)
            wave(i, n, parts[n])
        score(i)
        if i == 0:
            pl.semaphore_wait(barrier, feats + 1)
        send_scores(i)

    def proj_copy(i, owner, to):
        place = proj.at[i, share_rows(owner), :]
        return copy(place, place, s2.at[i, to], r2.at[i, owner], "feat", to)

    for i in range(pieces):
        total = scores[i, share_rows(me), :]
        for source in others:
            score_copy(i, me, source, source).wait_recv()
            total = total + score_recv[i, source]
        proj[i, share_rows(me), :] = total * (1.0 / math.sqrt(width * feats))
        for to in others:
            proj_copy(i, me, to).start()

    def upd_copy(stage, to):
        source = (upd.at[1 - core], pair)[stage]
        return copy(source, upd_recv.at[stage], s3.at[stage], r3.at[stage], "samp", to)

    for i in range(pieces):
        for source in others:
            proj_copy(i, source, source).wait_recv()
        low = proj[i].astype(jnp.bfloat16)
        for q in range(2):
            term = jnp.dot(
                low, features[piece_rows(i), half_cols(q)],
                preferred_element_type=jnp.float32,
            )
            upd[q] = upd[q] + term if i else term

    upd_copy(0, sibling).start()
    upd_copy(0, sibling).wait_recv()
    pair[...] = upd[core] + upd_recv[0]
    upd_copy(1, partner).start()
    upd_copy(1, partner).wait_recv()
    total = pair[...] + upd_recv[1]
    block = basis[core] + total * (1.0 / math.sqrt(rows * samps))
    grown[core] = block
    gram = lax.dot_general(
        block, block, (((1,), (1,)), ((), ())), precision=HIGHEST,
        preferred_element_type=jnp.float32,
    )
    halves[0] = jnp.concatenate([gram[: order // 2], gram[order // 2 :]], axis=1)
    half_copy = copy(halves.at[0], halves.at[1], s4.at[0], r4.at[0], "samp", sibling)
    half_copy.start()

    def grown_copy(which):
        return copy(grown.at[which], grown.at[which], s4.at[1], r4.at[1], "samp", sibling)

    grown_copy(core).start()
    half_copy.wait_recv()
    grams[me] = halves[0] + halves[1]

    def gram_copy(slot, to):
        return copy(grams.at[slot], grams.at[slot], s5.at[to], r5.at[slot], "feat", to)

    for to in others:
        gram_copy(me, to).start()
    grown_copy(1 - core).wait_recv()
    for to in others:
        for i in range(pieces):
            score_copy(i, to, me, to).wait_send()
            proj_copy(i, me, to).wait_send()
    upd_copy(0, sibling).wait_send()
    upd_copy(1, partner).wait_send()
    half_copy.wait_send()
    grown_copy(core).wait_send()
    for source in others:
        gram_copy(source, source).wait_recv()
    packed = grams[0]
    for slot in range(1, feats):
        packed = packed + grams[slot]
    gram_out[...] = packed * (1.0 / (width * feats))
    for to in others:
        gram_copy(me, to).wait_send()


def finish(proj, grown, packed, out, scores_out, result, out_sems, score_sems):
    pieces, order, chunk = proj.shape
    parts, _, span = grown.shape
    stores = [
        pltpu.make_async_copy(
            proj.at[slot], scores_out.at[:, slot * chunk : (slot + 1) * chunk],
            score_sems.at[slot],
        )
        for slot in range(pieces)
    ]
    for store in stores:
        store.start()
    halves = packed[...]
    gram = jnp.concatenate([halves[:, :order], halves[:, order:]], axis=0)
    inverse = inverse_factor(gram)
    high, middle, low = split(inverse)
    left = jnp.concatenate([high, high, middle, high, middle, low], axis=1)
    for q in range(parts):
        high, middle, low = split(grown[q])
        right = jnp.concatenate([high, middle, high, low, middle, high], axis=0)
        result[q] = jnp.dot(left, right, preferred_element_type=jnp.float32)
        store = pltpu.make_async_copy(
            result.at[q], out.at[:, q * span : (q + 1) * span], out_sems.at[q]
        )
        store.start()
        stores.append(store)
    for store in stores:
        store.wait()


def fused(feats, samps, embeddings, sign_bits, perms, gauss, scale, phase, basis):
    rows, width = embeddings.shape
    order = basis.shape[0]
    pieces, half, share = rows // BLOCK, width // 2, order // feats
    line = (1, width)
    whole = pl.BlockSpec(memory_space=pltpu.VMEM)
    far = pl.BlockSpec(memory_space=pltpu.HBM)
    f32, bf16, dma = jnp.float32, jnp.bfloat16, pltpu.SemaphoreType.DMA
    packed = (order // 2, 2 * order)
    operands = (
        embeddings, sign_bits.reshape(line), perms.reshape(line), gauss.reshape(line),
        scale.reshape(line), phase.reshape(line), basis,
    )
    near = pl.pallas_call(
        functools.partial(kernel, feats, samps),
        out_shape=(
            pltpu.VMEM((pieces, order, BLOCK), f32),
            pltpu.VMEM((2, order, half), f32),
            pltpu.VMEM(packed, f32),
        ),
        in_specs=[far] * 7,
        out_specs=(whole, whole, whole),
        scratch_shapes=[
            pltpu.VMEM((rows, width), bf16),
            pltpu.VMEM(line, jnp.int32),
            pltpu.VMEM(line, jnp.int32),
            pltpu.VMEM(line, f32),
            pltpu.VMEM(line, f32),
            pltpu.VMEM(line, f32),
            pltpu.VMEM((2, order, half), f32),
            pltpu.VMEM((width, width), bf16),
            pltpu.VMEM((BLOCK, BLOCK), bf16),
            pltpu.VMEM((rows, width), bf16),
            pltpu.VMEM((BLOCK, width), bf16),
            pltpu.VMEM((BLOCK, width), bf16),
            pltpu.VMEM((pieces, order, BLOCK), f32),
            pltpu.VMEM((pieces, feats, share, BLOCK), f32),
            pltpu.VMEM((2, order, half), f32),
            pltpu.VMEM((2, order, half), f32),
            pltpu.VMEM((order, half), f32),
            pltpu.VMEM((2,) + packed, f32),
            pltpu.VMEM((feats,) + packed, f32),
        ]
        + [dma((pieces, feats))] * 4
        + [dma((2,))] * 4
        + [dma((feats,))] * 2
        + [dma((7,)), dma((pieces,))],
        compiler_params=pltpu.CompilerParams(
            collective_id=0, has_side_effects=True, vmem_limit_bytes=48 << 20
        ),
        name="oja",
    )(*[pltpu.with_memory_space_constraint(x, pltpu.HBM) for x in operands])
    near = [pltpu.with_memory_space_constraint(x, pltpu.VMEM) for x in near]
    return pl.pallas_call(
        finish,
        out_shape=(
            jax.ShapeDtypeStruct((order, width), f32),
            jax.ShapeDtypeStruct((order, rows), f32),
        ),
        in_specs=[whole] * 3,
        out_specs=(far, far),
        scratch_shapes=[pltpu.VMEM((2, order, half), f32), dma((2,)), dma((pieces,))],
        compiler_params=pltpu.CompilerParams(vmem_limit_bytes=16 << 20),
        name="finish",
    )(*near)


def sylvester(width):
    indices = lax.iota(jnp.int32, width)
    return parity_sign(indices[:, None] & indices[None, :]).astype(jnp.bfloat16)


def general(embeddings, sign_bits, perms, gauss, scale, phase, basis):
    rows, width = embeddings.shape
    table = sylvester(width)
    features_total = width * lax.axis_size("feat")
    span_total = rows * lax.axis_size("samp")
    signs = (2 * sign_bits - 1).astype(jnp.bfloat16)
    columns = parity_sign(lax.iota(jnp.int32, width)[:, None] & perms[0][None, :]).astype(
        jnp.bfloat16
    )
    first = jnp.dot(embeddings * signs, columns, preferred_element_type=jnp.float32)
    mixed = (first.astype(jnp.bfloat16) * gauss).astype(jnp.bfloat16)
    freq = jnp.dot(mixed, table, preferred_element_type=jnp.float32) * scale / width + phase
    features = (math.sqrt(2.0) * jnp.cos(freq)).astype(jnp.bfloat16)
    partial_scores = lax.dot_general(
        basis.astype(jnp.bfloat16), features, (((1,), (1,)), ((), ())),
        preferred_element_type=jnp.float32,
    )
    projections = lax.psum(partial_scores, "feat") / math.sqrt(features_total)
    update_part = jnp.dot(
        projections.astype(jnp.bfloat16), features, preferred_element_type=jnp.float32
    )
    grown = basis + lax.psum(update_part, "samp") / math.sqrt(span_total)
    gram = lax.psum(jnp.dot(grown, grown.T, precision=HIGHEST), "feat")
    lower = jnp.linalg.cholesky(gram / features_total)
    return jax.scipy.linalg.solve_triangular(lower, grown, lower=True), projections


def solution(mesh):
    feats, samps = mesh.shape["feat"], mesh.shape["samp"]

    def local(embeddings, sign_bits, perms, gauss, scale, phase, basis):
        rows, width = embeddings.shape
        fits = (
            rows % BLOCK == 0
            and width % (2 * BLOCK) == 0
            and perms.shape[0] == 1
            and basis.shape[0] == 64
            and feats in (2, 4, 8)
            and samps == 4
            and rows >= 2 * BLOCK
        )
        body = functools.partial(fused, feats, samps) if fits else general
        return body(embeddings, sign_bits, perms, gauss, scale, phase, basis)

    placed = (
        P(("grp", "samp"), None),
        P("feat"),
        P("feat", None),
        P("feat"),
        P("feat"),
        P("feat"),
        P("grp", "feat"),
    )
    return jax.shard_map(
        local,
        mesh=mesh,
        in_specs=placed,
        out_specs=(P("grp", "feat"), P("grp", "samp")),
        check_vma=False,
    )
```

```python
import functools
import math

import jax
import jax.numpy as jnp
import numpy as np
from jax import lax
from jax.experimental import pallas as pl
from jax.experimental.pallas import tpu as pltpu
from jax.sharding import PartitionSpec as P

MESH = pl.DeviceIdType.MESH
BLOCK = 256
TAIL = 128
HIGHEST = lax.Precision.HIGHEST


def cosine_coefficients(degree):
    nodes = np.cos(np.pi * (np.arange(400) + 0.5) / 400)
    squares = (nodes + 1) / 8
    fitted = np.polynomial.Chebyshev.fit(
        squares, np.cos(2 * np.pi * np.sqrt(squares)), degree, domain=[0, 0.25]
    )
    return [float(c) * math.sqrt(2.0) for c in fitted.convert(kind=np.polynomial.Polynomial).coef]


COS = cosine_coefficients(5)


def parity_sign(bits):
    for shift in (8, 4, 2, 1):
        bits = bits ^ jnp.right_shift(bits, shift)
    return (1 - 2 * (bits & 1)).astype(jnp.float32)


def scaled_cosine(turns):
    rest = turns - jnp.round(turns)
    square = rest * rest
    total = jnp.full_like(square, COS[-1])
    for c in COS[-2::-1]:
        total = total * square + c
    return total


def transform(blocks):
    stride = 1
    while stride < len(blocks):
        result = list(blocks)
        for i in range(len(blocks)):
            if not i & stride:
                result[i] = blocks[i] + blocks[i + stride]
                result[i + stride] = blocks[i] - blocks[i + stride]
        blocks = result
        stride *= 2
    return blocks


def split(x):
    high = x.astype(jnp.bfloat16)
    rest = x - high.astype(jnp.float32)
    middle = rest.astype(jnp.bfloat16)
    low = (rest - middle.astype(jnp.float32)).astype(jnp.bfloat16)
    return high, middle, low


def inverse_factor(gram):
    size = gram.shape[0]
    row = lax.broadcasted_iota(jnp.int32, (8, size), 0)
    lane = lax.broadcasted_iota(jnp.int32, (8, size), 1)
    width = 2 * size
    sub = lax.broadcasted_iota(jnp.int32, (8, width), 0)
    groups = [
        jnp.concatenate(
            [(lane == row + 8 * g).astype(jnp.float32), gram[8 * g : 8 * g + 8]], axis=1
        )
        for g in range(size // 8)
    ]
    pivots = [jnp.ones((8, width), jnp.float32) for _ in groups]
    step = 8

    def spread(x):
        return jnp.broadcast_to(x, (8, width))

    for own in range(size // 8):
        first = size + own * step
        live = range(own, size // 8)
        rows = [spread(groups[own][k : k + 1]) for k in range(step)]
        cols = [
            {g: spread(groups[g][:, first + k : first + k + 1]) for g in live}
            for k in range(step)
        ]
        cross = {
            (k, m): spread(cols[m][own][k : k + 1]) for k in range(step) for m in range(k + 1)
        }
        for k in range(step):
            if k % 2:
                inverse = ahead
            else:
                inverse = 1.0 / cross[k, k]
                minor = cross[k, k] * cross[k + 1, k + 1] - cross[k + 1, k] * cross[k + 1, k]
                ahead = cross[k, k] / minor
            pivots[own] = jnp.where(sub == k, cross[k, k], pivots[own])
            factor = {later: cross[later, k] * inverse for later in range(k + 1, step)}
            for later in range(k + 1, step):
                for m in range(k + 1, later + 1):
                    cross[later, m] = cross[later, m] - factor[later] * cross[m, k]
            for later in range(k + 1, step):
                rows[later] = rows[later] - factor[later] * rows[k]
                for g in live:
                    cols[later][g] = cols[later][g] - factor[later] * cols[k][g]
            for g in live:
                weight = cols[k][g] * inverse
                if g == own:
                    weight = jnp.where(sub > k, weight, 0.0)
                groups[g] = groups[g] - weight * rows[k]
    scaled = [g / jnp.sqrt(p) for g, p in zip(groups, pivots)]
    return jnp.concatenate(scaled, axis=0)[:, :size]


def kernel(
    feats, samps, emb_in, bits_in, perm_in, gauss_in, scale_in, phase_in, basis_in,
    proj, grown, gram_out,
    emb, bits, perm, gauss, scale, phase, basis,
    table, small, features, even, odd, scores, score_recv,
    upd, upd_recv, pair, halves, grams,
    s1, r1, s2, r2, s3, r3, s4, r4, s5, r5, loads, emb_loads,
):
    me = lax.axis_index("feat")
    my = lax.axis_index("samp")
    rows, width = emb.shape
    order = basis.shape[1]
    pieces = rows // BLOCK
    share = order // feats
    cuts = [(i, 0, BLOCK) for i in range(pieces - 1)]
    cuts += [(pieces - 1, k * TAIL, TAIL) for k in range(BLOCK // TAIL)]
    half = width // 2
    core = lax.rem(my, 2)
    sibling = my + 1 - 2 * core
    partner = lax.rem(my + 2, samps)
    blocks = width // BLOCK

    def piece_rows(i):
        return slice(i * BLOCK, (i + 1) * BLOCK)

    def share_rows(owner):
        return pl.ds(pl.multiple_of(owner * share, share), share)

    def half_cols(which):
        return slice(which * half, (which + 1) * half)

    def drain(place, sem):
        pltpu.make_async_copy(place, place, sem).wait()

    emb_copies = [
        pltpu.make_async_copy(
            emb_in.at[piece_rows(i), :], emb.at[piece_rows(i), :], emb_loads.at[i]
        )
        for i in range(pieces)
    ]
    pairs = (
        (perm_in, perm, 0), (bits_in, bits, 1), (gauss_in, gauss, 2), (scale_in, scale, 3),
        (phase_in, phase, 4), (basis_in.at[:, half_cols(0)], basis.at[0], 5),
        (basis_in.at[:, half_cols(1)], basis.at[1], 5),
    )
    parameters = [
        pltpu.make_async_copy(source, place, loads.at[n]) for source, place, n in pairs
    ]
    for load in parameters[:-2]:
        load.start()
    emb_copies[0].start()
    for load in parameters[-2:]:
        load.start()
    for load in emb_copies[1:]:
        load.start()
    barrier = pltpu.get_barrier_semaphore()
    others = [lax.rem(me + d, feats) for d in range(1, feats)]
    for to in others:
        pl.semaphore_signal(barrier, inc=1, device_id={"feat": to}, device_id_type=MESH)
    for to in (sibling, partner):
        pl.semaphore_signal(barrier, inc=1, device_id={"samp": to}, device_id_type=MESH)

    square = (BLOCK, BLOCK)
    small[...] = parity_sign(
        lax.broadcasted_iota(jnp.int32, square, 0) & lax.broadcasted_iota(jnp.int32, square, 1)
    ).astype(jnp.bfloat16)
    parameters[0].wait()
    places = perm[...]
    base = parity_sign(lax.broadcasted_iota(jnp.int32, (128, width), 0) & places & 127).astype(
        jnp.bfloat16
    )
    for a in range(width // 128):
        flips = parity_sign(jnp.right_shift(places, 7) & a).astype(jnp.bfloat16)
        table[a * 128 : (a + 1) * 128, :] = base * flips
    for load in parameters[1:-2]:
        load.wait()
    signs = (2 * bits[...] - 1).astype(jnp.float32).astype(jnp.bfloat16)
    gains = gauss[...]
    rate = scale[...] * (1.0 / (2.0 * math.pi * width))
    offset = phase[...] * (1.0 / (2.0 * math.pi))

    def copy(src, dst, send, recv, axis, to):
        return pltpu.make_async_remote_copy(
            src_ref=src, dst_ref=dst, send_sem=send, recv_sem=recv,
            device_id={axis: to}, device_id_type=MESH,
        )

    mixes = (even, odd)

    def mix(i, n):
        cols = slice(n * BLOCK, (n + 1) * BLOCK)
        signed = emb[piece_rows(i), :] * signs
        first = jnp.dot(signed, table[:, cols], preferred_element_type=jnp.float32)
        first = first.astype(jnp.bfloat16).astype(jnp.float32)
        mixes[i % 2][:, cols] = (first * gains[:, cols]).astype(jnp.bfloat16)

    def second(i, first, size):
        mixed = mixes[i % 2]
        return transform([
            jnp.dot(
                mixed[first : first + size, n * BLOCK : (n + 1) * BLOCK], small[...],
                preferred_element_type=jnp.float32,
            )
            for n in range(blocks)
        ])

    def wave(where, n, part):
        cols = slice(n * BLOCK, (n + 1) * BLOCK)
        turns = part * rate[:, cols] + offset[:, cols]
        features[where, cols] = scaled_cosine(turns).astype(jnp.bfloat16)

    def cut_rows(cut):
        i, first, size = cut
        return slice(i * BLOCK + first, i * BLOCK + first + size)

    def cut_cols(cut):
        return slice(cut[1], cut[1] + cut[2])

    def score(cut, basis_low):
        scores[cut[0], :, cut_cols(cut)] = lax.dot_general(
            basis_low, features[cut_rows(cut), :], (((1,), (1,)), ((), ())),
            preferred_element_type=jnp.float32,
        )

    def score_copy(n, owner, source, to):
        i, cols = cuts[n][0], cut_cols(cuts[n])
        return copy(
            scores.at[i, share_rows(owner), cols], score_recv.at[i, source, :, cols],
            s1.at[0], r1.at[n], "feat", to,
        )

    emb_copies[0].wait()
    for n in range(blocks):
        mix(0, n)
    for n, cut in enumerate(cuts):
        i, first, size = cut
        if i + 1 < pieces:
            emb_copies[i + 1].wait()
        parts = second(*cut)
        for m in range(blocks):
            if i + 1 < pieces:
                mix(i + 1, m)
            wave(cut_rows(cut), m, parts[m])
        if n == 0:
            drain(basis, loads.at[5])
            basis_low = jnp.concatenate([basis[0], basis[1]], axis=1).astype(jnp.bfloat16)
        score(cut, basis_low)
        if n == 0:
            pl.semaphore_wait(barrier, feats + 1)
        for to in others:
            score_copy(n, to, me, to).start()

    def proj_copy(n, owner, to):
        place = proj.at[cuts[n][0], share_rows(owner), cut_cols(cuts[n])]
        return copy(place, place, s2.at[0], r2.at[n], "feat", to)

    for n, cut in enumerate(cuts):
        i, cols = cut[0], cut_cols(cut)
        total = scores[i, share_rows(me), cols]
        drain(score_recv.at[i, 1:feats, :, cols], r1.at[n])
        for source in others:
            total = total + score_recv[i, source, :, cols]
        proj[i, share_rows(me), cols] = total * (1.0 / math.sqrt(width * feats))
        for to in others:
            proj_copy(n, me, to).start()

    def upd_copy(stage, to):
        source = (upd.at[1 - core], pair)[stage]
        return copy(source, upd_recv.at[stage], s3.at[stage], r3.at[stage], "samp", to)

    for n, cut in enumerate(cuts):
        drain(proj.at[cut[0], share:order, cut_cols(cut)], r2.at[n])
        low = proj[cut[0], :, cut_cols(cut)].astype(jnp.bfloat16)
        for q in range(2):
            term = jnp.dot(
                low, features[cut_rows(cut), half_cols(q)],
                preferred_element_type=jnp.float32,
            )
            upd[q] = upd[q] + term if n else term

    upd_copy(0, sibling).start()
    upd_copy(0, sibling).wait_recv()
    pair[...] = upd[core] + upd_recv[0]
    upd_copy(1, partner).start()
    upd_copy(1, partner).wait_recv()
    total = pair[...] + upd_recv[1]
    block = basis[core] + total * (1.0 / math.sqrt(rows * samps))
    grown[core] = block
    gram = lax.dot_general(
        block, block, (((1,), (1,)), ((), ())), precision=HIGHEST,
        preferred_element_type=jnp.float32,
    )
    halves[0] = jnp.concatenate([gram[: order // 2], gram[order // 2 :]], axis=1)
    half_copy = copy(halves.at[0], halves.at[1], s4.at[0], r4.at[0], "samp", sibling)
    half_copy.start()

    def grown_copy(which):
        return copy(grown.at[which], grown.at[which], s4.at[1], r4.at[1], "samp", sibling)

    grown_copy(core).start()
    half_copy.wait_recv()
    grams[me] = halves[0] + halves[1]

    def gram_copy(slot, to):
        return copy(grams.at[slot], grams.at[slot], s5.at[0], r5.at[0], "feat", to)

    for to in others:
        gram_copy(me, to).start()
    grown_copy(1 - core).wait_recv()
    drain(score_recv.at[:, 1:feats], s1.at[0])
    drain(proj.at[:, share:order, :], s2.at[0])
    upd_copy(0, sibling).wait_send()
    upd_copy(1, partner).wait_send()
    half_copy.wait_send()
    grown_copy(core).wait_send()
    drain(grams.at[1:feats], r5.at[0])
    packed = grams[0]
    for slot in range(1, feats):
        packed = packed + grams[slot]
    gram_out[...] = packed * (1.0 / (width * feats))
    drain(grams.at[1:feats], s5.at[0])


def finish(proj, grown, packed, out, scores_out, result, out_sems, score_sems):
    pieces, order, chunk = proj.shape
    parts, _, span = grown.shape
    stores = [
        pltpu.make_async_copy(
            proj.at[slot], scores_out.at[:, slot * chunk : (slot + 1) * chunk],
            score_sems.at[0],
        )
        for slot in range(pieces)
    ]
    for store in stores:
        store.start()
    halves = packed[...]
    gram = jnp.concatenate([halves[:, :order], halves[:, order:]], axis=0)
    inverse = inverse_factor(gram)
    high, middle, low = split(inverse)
    left = jnp.concatenate([high, high, middle, high, middle, low], axis=1)
    for q in range(parts):
        high, middle, low = split(grown[q])
        right = jnp.concatenate([high, middle, high, low, middle, high], axis=0)
        result[q] = jnp.dot(left, right, preferred_element_type=jnp.float32)
        store = pltpu.make_async_copy(
            result.at[q], out.at[:, q * span : (q + 1) * span], out_sems.at[0]
        )
        store.start()
    for place, sem in ((proj, score_sems.at[0]), (result, out_sems.at[0])):
        pltpu.make_async_copy(place, place, sem).wait()


def fused(feats, samps, embeddings, sign_bits, perms, gauss, scale, phase, basis):
    rows, width = embeddings.shape
    order = basis.shape[0]
    pieces, half, share = rows // BLOCK, width // 2, order // feats
    cuts = pieces - 1 + BLOCK // TAIL
    line = (1, width)
    whole = pl.BlockSpec(memory_space=pltpu.VMEM)
    far = pl.BlockSpec(memory_space=pltpu.HBM)
    f32, bf16, dma = jnp.float32, jnp.bfloat16, pltpu.SemaphoreType.DMA
    packed = (order // 2, 2 * order)
    operands = (
        embeddings, sign_bits.reshape(line), perms.reshape(line), gauss.reshape(line),
        scale.reshape(line), phase.reshape(line), basis,
    )
    near = pl.pallas_call(
        functools.partial(kernel, feats, samps),
        out_shape=(
            pltpu.VMEM((pieces, order, BLOCK), f32),
            pltpu.VMEM((2, order, half), f32),
            pltpu.VMEM(packed, f32),
        ),
        in_specs=[far] * 7,
        out_specs=(whole, whole, whole),
        scratch_shapes=[
            pltpu.VMEM((rows, width), bf16),
            pltpu.VMEM(line, jnp.int32),
            pltpu.VMEM(line, jnp.int32),
            pltpu.VMEM(line, f32),
            pltpu.VMEM(line, f32),
            pltpu.VMEM(line, f32),
            pltpu.VMEM((2, order, half), f32),
            pltpu.VMEM((width, width), bf16),
            pltpu.VMEM((BLOCK, BLOCK), bf16),
            pltpu.VMEM((rows, width), bf16),
            pltpu.VMEM((BLOCK, width), bf16),
            pltpu.VMEM((BLOCK, width), bf16),
            pltpu.VMEM((pieces, order, BLOCK), f32),
            pltpu.VMEM((pieces, feats, share, BLOCK), f32),
            pltpu.VMEM((2, order, half), f32),
            pltpu.VMEM((2, order, half), f32),
            pltpu.VMEM((order, half), f32),
            pltpu.VMEM((2,) + packed, f32),
            pltpu.VMEM((feats,) + packed, f32),
        ]
        + [dma((1,)), dma((cuts,))] * 2
        + [dma((2,))] * 4
        + [dma((1,))] * 2
        + [dma((6,)), dma((pieces,))],
        compiler_params=pltpu.CompilerParams(
            collective_id=0, has_side_effects=True, vmem_limit_bytes=48 << 20
        ),
        name="oja",
    )(*[pltpu.with_memory_space_constraint(x, pltpu.HBM) for x in operands])
    near = [pltpu.with_memory_space_constraint(x, pltpu.VMEM) for x in near]
    return pl.pallas_call(
        finish,
        out_shape=(
            jax.ShapeDtypeStruct((order, width), f32),
            jax.ShapeDtypeStruct((order, rows), f32),
        ),
        in_specs=[whole] * 3,
        out_specs=(far, far),
        scratch_shapes=[pltpu.VMEM((2, order, half), f32), dma((1,)), dma((1,))],
        compiler_params=pltpu.CompilerParams(vmem_limit_bytes=16 << 20),
        name="finish",
    )(*near)


def sylvester(width):
    indices = lax.iota(jnp.int32, width)
    return parity_sign(indices[:, None] & indices[None, :]).astype(jnp.bfloat16)


def general(embeddings, sign_bits, perms, gauss, scale, phase, basis):
    rows, width = embeddings.shape
    table = sylvester(width)
    features_total = width * lax.axis_size("feat")
    span_total = rows * lax.axis_size("samp")
    signs = (2 * sign_bits - 1).astype(jnp.bfloat16)
    columns = parity_sign(lax.iota(jnp.int32, width)[:, None] & perms[0][None, :]).astype(
        jnp.bfloat16
    )
    first = jnp.dot(embeddings * signs, columns, preferred_element_type=jnp.float32)
    mixed = (first.astype(jnp.bfloat16) * gauss).astype(jnp.bfloat16)
    freq = jnp.dot(mixed, table, preferred_element_type=jnp.float32) * scale / width + phase
    features = (math.sqrt(2.0) * jnp.cos(freq)).astype(jnp.bfloat16)
    partial_scores = lax.dot_general(
        basis.astype(jnp.bfloat16), features, (((1,), (1,)), ((), ())),
        preferred_element_type=jnp.float32,
    )
    projections = lax.psum(partial_scores, "feat") / math.sqrt(features_total)
    update_part = jnp.dot(
        projections.astype(jnp.bfloat16), features, preferred_element_type=jnp.float32
    )
    grown = basis + lax.psum(update_part, "samp") / math.sqrt(span_total)
    gram = lax.psum(jnp.dot(grown, grown.T, precision=HIGHEST), "feat")
    lower = jnp.linalg.cholesky(gram / features_total)
    return jax.scipy.linalg.solve_triangular(lower, grown, lower=True), projections


def solution(mesh):
    feats, samps = mesh.shape["feat"], mesh.shape["samp"]

    def local(embeddings, sign_bits, perms, gauss, scale, phase, basis):
        rows, width = embeddings.shape
        fits = (
            rows % BLOCK == 0
            and width % (2 * BLOCK) == 0
            and perms.shape[0] == 1
            and basis.shape[0] == 64
            and feats in (2, 4, 8)
            and samps == 4
            and rows >= 2 * BLOCK
        )
        body = functools.partial(fused, feats, samps) if fits else general
        return body(embeddings, sign_bits, perms, gauss, scale, phase, basis)

    placed = (
        P(("grp", "samp"), None),
        P("feat"),
        P("feat", None),
        P("feat"),
        P("feat"),
        P("feat"),
        P("grp", "feat"),
    )
    return jax.shard_map(
        local,
        mesh=mesh,
        in_specs=placed,
        out_specs=(P("grp", "feat"), P("grp", "samp")),
        check_vma=False,
    )
```

```python
import functools
import math

import jax
import jax.numpy as jnp
import numpy as np
from jax import lax
from jax.experimental import pallas as pl
from jax.experimental.pallas import tpu as pltpu
from jax.sharding import PartitionSpec as P

MESH = pl.DeviceIdType.MESH
BLOCK = 256
TAIL = 128
PASSED = 2
HIGHEST = lax.Precision.HIGHEST


def cosine_coefficients(degree):
    nodes = np.cos(np.pi * (np.arange(400) + 0.5) / 400)
    squares = (nodes + 1) / 8
    fitted = np.polynomial.Chebyshev.fit(
        squares, np.cos(2 * np.pi * np.sqrt(squares)), degree, domain=[0, 0.25]
    )
    return [float(c) * math.sqrt(2.0) for c in fitted.convert(kind=np.polynomial.Polynomial).coef]


COS = cosine_coefficients(5)


def parity_sign(bits):
    for shift in (8, 4, 2, 1):
        bits = bits ^ jnp.right_shift(bits, shift)
    return (1 - 2 * (bits & 1)).astype(jnp.float32)


def scaled_cosine(turns):
    rest = turns - jnp.round(turns)
    square = rest * rest
    total = jnp.full_like(square, COS[-1])
    for c in COS[-2::-1]:
        total = total * square + c
    return total


def transform(blocks):
    stride = 1
    while stride < len(blocks):
        result = list(blocks)
        for i in range(len(blocks)):
            if not i & stride:
                result[i] = blocks[i] + blocks[i + stride]
                result[i + stride] = blocks[i] - blocks[i + stride]
        blocks = result
        stride *= 2
    return blocks


def split(x):
    high = x.astype(jnp.bfloat16)
    rest = x - high.astype(jnp.float32)
    middle = rest.astype(jnp.bfloat16)
    low = (rest - middle.astype(jnp.float32)).astype(jnp.bfloat16)
    return high, middle, low


def inverse_factor(gram):
    size = gram.shape[0]
    row = lax.broadcasted_iota(jnp.int32, (8, size), 0)
    lane = lax.broadcasted_iota(jnp.int32, (8, size), 1)
    width = 2 * size
    sub = lax.broadcasted_iota(jnp.int32, (8, width), 0)
    groups = [
        jnp.concatenate(
            [(lane == row + 8 * g).astype(jnp.float32), gram[8 * g : 8 * g + 8]], axis=1
        )
        for g in range(size // 8)
    ]
    pivots = [jnp.ones((8, width), jnp.float32) for _ in groups]
    step = 8

    def spread(x):
        return jnp.broadcast_to(x, (8, width))

    for own in range(size // 8):
        first = size + own * step
        live = range(own, size // 8)
        rows = [spread(groups[own][k : k + 1]) for k in range(step)]
        cols = [
            {g: spread(groups[g][:, first + k : first + k + 1]) for g in live}
            for k in range(step)
        ]
        cross = {
            (k, m): spread(cols[m][own][k : k + 1]) for k in range(step) for m in range(k + 1)
        }
        for k in range(step):
            if k % 2:
                inverse = ahead
            else:
                inverse = 1.0 / cross[k, k]
                minor = cross[k, k] * cross[k + 1, k + 1] - cross[k + 1, k] * cross[k + 1, k]
                ahead = cross[k, k] / minor
            pivots[own] = jnp.where(sub == k, cross[k, k], pivots[own])
            factor = {later: cross[later, k] * inverse for later in range(k + 1, step)}
            for later in range(k + 1, step):
                for m in range(k + 1, later + 1):
                    cross[later, m] = cross[later, m] - factor[later] * cross[m, k]
            for later in range(k + 1, step):
                rows[later] = rows[later] - factor[later] * rows[k]
                for g in live:
                    cols[later][g] = cols[later][g] - factor[later] * cols[k][g]
            for g in live:
                weight = cols[k][g] * inverse
                if g == own:
                    weight = jnp.where(sub > k, weight, 0.0)
                groups[g] = groups[g] - weight * rows[k]
    scaled = [g / jnp.sqrt(p) for g, p in zip(groups, pivots)]
    return jnp.concatenate(scaled, axis=0)[:, :size]


def kernel(
    feats, samps, emb_in, bits_in, perm_in, gauss_in, scale_in, phase_in, basis_in,
    proj, grown, gram_out,
    emb, bits, perm, gauss, scale, phase, basis,
    table, small, features, even, odd, scores, score_recv,
    upd, upd_recv, pair, halves, grams,
    s1, r1, s2, r2, s3, r3, s4, r4, s5, r5, r6, loads, emb_loads,
):
    me = lax.axis_index("feat")
    my = lax.axis_index("samp")
    rows, width = emb.shape
    order = basis.shape[1]
    pieces = rows // BLOCK
    share = order // feats
    cuts = [(i, 0, BLOCK) for i in range(pieces - 1)]
    cuts += [(pieces - 1, k * TAIL, TAIL) for k in range(BLOCK // TAIL)]
    half = width // 2
    core = lax.rem(my, 2)
    sibling = my + 1 - 2 * core
    partner = lax.rem(my + 2, samps)
    blocks = width // BLOCK

    def piece_rows(i):
        return slice(i * BLOCK, (i + 1) * BLOCK)

    def share_rows(owner):
        return pl.ds(pl.multiple_of(owner * share, share), share)

    def half_cols(which):
        return slice(which * half, (which + 1) * half)

    def drain(place, sem):
        pltpu.make_async_copy(place, place, sem).wait()

    emb_copies = [
        pltpu.make_async_copy(
            emb_in.at[piece_rows(i), :], emb.at[piece_rows(i), :], emb_loads.at[i]
        )
        for i in range(pieces)
    ]
    pairs = (
        (perm_in, perm, 0), (bits_in, bits, 1), (gauss_in, gauss, 2), (scale_in, scale, 3),
        (phase_in, phase, 4), (basis_in.at[:, half_cols(0)], basis.at[0], 5),
        (basis_in.at[:, half_cols(1)], basis.at[1], 5),
    )
    parameters = [
        pltpu.make_async_copy(source, place, loads.at[n]) for source, place, n in pairs
    ]
    for load in parameters[:-2]:
        load.start()
    emb_copies[0].start()
    for load in parameters[-2:]:
        load.start()
    for load in emb_copies[1:]:
        load.start()
    barrier = pltpu.get_barrier_semaphore()
    mate = me + 1 - 2 * lax.rem(me, 2)
    across = lax.rem(me + 2, feats)
    opposite = lax.rem(mate + 2, feats)
    others = [opposite, across, mate]
    for to in others:
        pl.semaphore_signal(barrier, inc=1, device_id={"feat": to}, device_id_type=MESH)
    for to in (sibling, partner):
        pl.semaphore_signal(barrier, inc=1, device_id={"samp": to}, device_id_type=MESH)

    square = (BLOCK, BLOCK)
    small[...] = parity_sign(
        lax.broadcasted_iota(jnp.int32, square, 0) & lax.broadcasted_iota(jnp.int32, square, 1)
    ).astype(jnp.bfloat16)
    parameters[0].wait()
    places = perm[...]
    base = parity_sign(lax.broadcasted_iota(jnp.int32, (128, width), 0) & places & 127).astype(
        jnp.bfloat16
    )
    for a in range(width // 128):
        flips = parity_sign(jnp.right_shift(places, 7) & a).astype(jnp.bfloat16)
        table[a * 128 : (a + 1) * 128, :] = base * flips
    for load in parameters[1:-2]:
        load.wait()
    signs = (2 * bits[...] - 1).astype(jnp.float32).astype(jnp.bfloat16)
    gains = gauss[...]
    rate = scale[...] * (1.0 / (2.0 * math.pi * width))
    offset = phase[...] * (1.0 / (2.0 * math.pi))

    def copy(src, dst, send, recv, axis, to):
        return pltpu.make_async_remote_copy(
            src_ref=src, dst_ref=dst, send_sem=send, recv_sem=recv,
            device_id={axis: to}, device_id_type=MESH,
        )

    mixes = (even, odd)

    def mix(i, n):
        cols = slice(n * BLOCK, (n + 1) * BLOCK)
        signed = emb[piece_rows(i), :] * signs
        first = jnp.dot(signed, table[:, cols], preferred_element_type=jnp.float32)
        first = first.astype(jnp.bfloat16).astype(jnp.float32)
        mixes[i % 2][:, cols] = (first * gains[:, cols]).astype(jnp.bfloat16)

    def second(i, first, size):
        mixed = mixes[i % 2]
        return transform([
            jnp.dot(
                mixed[first : first + size, n * BLOCK : (n + 1) * BLOCK], small[...],
                preferred_element_type=jnp.float32,
            )
            for n in range(blocks)
        ])

    def wave(where, n, part):
        cols = slice(n * BLOCK, (n + 1) * BLOCK)
        turns = part * rate[:, cols] + offset[:, cols]
        features[where, cols] = scaled_cosine(turns).astype(jnp.bfloat16)

    def cut_rows(cut):
        i, first, size = cut
        return slice(i * BLOCK + first, i * BLOCK + first + size)

    def cut_cols(cut):
        return slice(cut[1], cut[1] + cut[2])

    def score(cut, basis_low):
        scores[cut[0], :, cut_cols(cut)] = lax.dot_general(
            basis_low, features[cut_rows(cut), :], (((1,), (1,)), ((), ())),
            preferred_element_type=jnp.float32,
        )

    def score_copy(n, owner, source, to):
        i, cols = cuts[n][0], cut_cols(cuts[n])
        return copy(
            scores.at[i, share_rows(owner), cols], score_recv.at[i, source, :, cols],
            s1.at[0], r1.at[n], "feat", to,
        )

    emb_copies[0].wait()
    for n in range(blocks):
        mix(0, n)
    for n, cut in enumerate(cuts):
        i, first, size = cut
        if i + 1 < pieces:
            emb_copies[i + 1].wait()
        parts = second(*cut)
        for m in range(blocks):
            if i + 1 < pieces:
                mix(i + 1, m)
            wave(cut_rows(cut), m, parts[m])
        if n == 0:
            drain(basis, loads.at[5])
            basis_low = jnp.concatenate([basis[0], basis[1]], axis=1).astype(jnp.bfloat16)
        score(cut, basis_low)
        if n == 0:
            pl.semaphore_wait(barrier, feats + 1)
        for to in others:
            score_copy(n, to, me, to).start()

    def proj_copy(n, owner, to):
        place = proj.at[cuts[n][0], share_rows(owner), cut_cols(cuts[n])]
        return copy(place, place, s2.at[0], r2.at[n], "feat", to)

    def across_copy(n, owner):
        place = proj.at[cuts[n][0], share_rows(owner), cut_cols(cuts[n])]
        return copy(place, place, s2.at[0], r6.at[n], "feat", across)

    def pass_on(n):
        across_copy(n, across).wait_recv()
        proj_copy(n, across, mate).start()

    def add_all(n):
        i, cols = cuts[n][0], cut_cols(cuts[n])
        total = scores[i, share_rows(me), cols]
        drain(score_recv.at[i, 1:feats, :, cols], r1.at[n])
        for source in others:
            total = total + score_recv[i, source, :, cols]
        proj[i, share_rows(me), cols] = total * (1.0 / math.sqrt(width * feats))
        if n < PASSED:
            across_copy(n, me).start()
            proj_copy(n, me, mate).start()
            return
        for to in others:
            proj_copy(n, me, to).start()

    for n in range(len(cuts)):
        add_all(n)
    for n in range(PASSED):
        pass_on(n)

    def upd_copy(stage, to):
        source = (upd.at[1 - core], pair)[stage]
        return copy(source, upd_recv.at[stage], s3.at[stage], r3.at[stage], "samp", to)

    for n, cut in enumerate(cuts):
        late = 2 if n < PASSED else 1
        drain(proj.at[cut[0], late * share : order, cut_cols(cut)], r2.at[n])
        low = proj[cut[0], :, cut_cols(cut)].astype(jnp.bfloat16)
        for q in range(2):
            term = jnp.dot(
                low, features[cut_rows(cut), half_cols(q)],
                preferred_element_type=jnp.float32,
            )
            upd[q] = upd[q] + term if n else term

    upd_copy(0, sibling).start()
    upd_copy(0, sibling).wait_recv()
    pair[...] = upd[core] + upd_recv[0]
    upd_copy(1, partner).start()
    upd_copy(1, partner).wait_recv()
    total = pair[...] + upd_recv[1]
    block = basis[core] + total * (1.0 / math.sqrt(rows * samps))
    grown[core] = block
    gram = lax.dot_general(
        block, block, (((1,), (1,)), ((), ())), precision=HIGHEST,
        preferred_element_type=jnp.float32,
    )
    halves[0] = jnp.concatenate([gram[: order // 2], gram[order // 2 :]], axis=1)
    half_copy = copy(halves.at[0], halves.at[1], s4.at[0], r4.at[0], "samp", sibling)
    half_copy.start()

    def grown_copy(which):
        return copy(grown.at[which], grown.at[which], s4.at[1], r4.at[1], "samp", sibling)

    grown_copy(core).start()
    half_copy.wait_recv()
    grams[me] = halves[0] + halves[1]

    def gram_copy(slot, to):
        return copy(grams.at[slot], grams.at[slot], s5.at[0], r5.at[0], "feat", to)

    for to in others:
        gram_copy(me, to).start()
    grown_copy(1 - core).wait_recv()
    drain(score_recv.at[:, 1:feats], s1.at[0])
    drain(proj.at[:, share:order, :], s2.at[0])
    upd_copy(0, sibling).wait_send()
    upd_copy(1, partner).wait_send()
    half_copy.wait_send()
    grown_copy(core).wait_send()
    drain(grams.at[1:feats], r5.at[0])
    packed = grams[0]
    for slot in range(1, feats):
        packed = packed + grams[slot]
    gram_out[...] = packed * (1.0 / (width * feats))
    drain(grams.at[1:feats], s5.at[0])


def finish(proj, grown, packed, out, scores_out, result, out_sems, score_sems):
    pieces, order, chunk = proj.shape
    parts, _, span = grown.shape
    stores = [
        pltpu.make_async_copy(
            proj.at[slot], scores_out.at[:, slot * chunk : (slot + 1) * chunk],
            score_sems.at[0],
        )
        for slot in range(pieces)
    ]
    for store in stores:
        store.start()
    halves = packed[...]
    gram = jnp.concatenate([halves[:, :order], halves[:, order:]], axis=0)
    inverse = inverse_factor(gram)
    high, middle, low = split(inverse)
    left = jnp.concatenate([high, high, middle, high, middle, low], axis=1)
    for q in range(parts):
        high, middle, low = split(grown[q])
        right = jnp.concatenate([high, middle, high, low, middle, high], axis=0)
        result[q] = jnp.dot(left, right, preferred_element_type=jnp.float32)
        store = pltpu.make_async_copy(
            result.at[q], out.at[:, q * span : (q + 1) * span], out_sems.at[0]
        )
        store.start()
    for place, sem in ((proj, score_sems.at[0]), (result, out_sems.at[0])):
        pltpu.make_async_copy(place, place, sem).wait()


def fused(feats, samps, embeddings, sign_bits, perms, gauss, scale, phase, basis):
    rows, width = embeddings.shape
    order = basis.shape[0]
    pieces, half, share = rows // BLOCK, width // 2, order // feats
    cuts = pieces - 1 + BLOCK // TAIL
    line = (1, width)
    whole = pl.BlockSpec(memory_space=pltpu.VMEM)
    far = pl.BlockSpec(memory_space=pltpu.HBM)
    f32, bf16, dma = jnp.float32, jnp.bfloat16, pltpu.SemaphoreType.DMA
    packed = (order // 2, 2 * order)
    operands = (
        embeddings, sign_bits.reshape(line), perms.reshape(line), gauss.reshape(line),
        scale.reshape(line), phase.reshape(line), basis,
    )
    near = pl.pallas_call(
        functools.partial(kernel, feats, samps),
        out_shape=(
            pltpu.VMEM((pieces, order, BLOCK), f32),
            pltpu.VMEM((2, order, half), f32),
            pltpu.VMEM(packed, f32),
        ),
        in_specs=[far] * 7,
        out_specs=(whole, whole, whole),
        scratch_shapes=[
            pltpu.VMEM((rows, width), bf16),
            pltpu.VMEM(line, jnp.int32),
            pltpu.VMEM(line, jnp.int32),
            pltpu.VMEM(line, f32),
            pltpu.VMEM(line, f32),
            pltpu.VMEM(line, f32),
            pltpu.VMEM((2, order, half), f32),
            pltpu.VMEM((width, width), bf16),
            pltpu.VMEM((BLOCK, BLOCK), bf16),
            pltpu.VMEM((rows, width), bf16),
            pltpu.VMEM((BLOCK, width), bf16),
            pltpu.VMEM((BLOCK, width), bf16),
            pltpu.VMEM((pieces, order, BLOCK), f32),
            pltpu.VMEM((pieces, feats, share, BLOCK), f32),
            pltpu.VMEM((2, order, half), f32),
            pltpu.VMEM((2, order, half), f32),
            pltpu.VMEM((order, half), f32),
            pltpu.VMEM((2,) + packed, f32),
            pltpu.VMEM((feats,) + packed, f32),
        ]
        + [dma((1,)), dma((cuts,))] * 2
        + [dma((2,))] * 4
        + [dma((1,))] * 2
        + [dma((PASSED,)), dma((6,)), dma((pieces,))],
        compiler_params=pltpu.CompilerParams(
            collective_id=0, has_side_effects=True, vmem_limit_bytes=48 << 20
        ),
        name="oja",
    )(*[pltpu.with_memory_space_constraint(x, pltpu.HBM) for x in operands])
    near = [pltpu.with_memory_space_constraint(x, pltpu.VMEM) for x in near]
    return pl.pallas_call(
        finish,
        out_shape=(
            jax.ShapeDtypeStruct((order, width), f32),
            jax.ShapeDtypeStruct((order, rows), f32),
        ),
        in_specs=[whole] * 3,
        out_specs=(far, far),
        scratch_shapes=[pltpu.VMEM((2, order, half), f32), dma((1,)), dma((1,))],
        compiler_params=pltpu.CompilerParams(vmem_limit_bytes=16 << 20),
        name="finish",
    )(*near)


def sylvester(width):
    indices = lax.iota(jnp.int32, width)
    return parity_sign(indices[:, None] & indices[None, :]).astype(jnp.bfloat16)


def general(embeddings, sign_bits, perms, gauss, scale, phase, basis):
    rows, width = embeddings.shape
    table = sylvester(width)
    features_total = width * lax.axis_size("feat")
    span_total = rows * lax.axis_size("samp")
    signs = (2 * sign_bits - 1).astype(jnp.bfloat16)
    columns = parity_sign(lax.iota(jnp.int32, width)[:, None] & perms[0][None, :]).astype(
        jnp.bfloat16
    )
    first = jnp.dot(embeddings * signs, columns, preferred_element_type=jnp.float32)
    mixed = (first.astype(jnp.bfloat16) * gauss).astype(jnp.bfloat16)
    freq = jnp.dot(mixed, table, preferred_element_type=jnp.float32) * scale / width + phase
    features = (math.sqrt(2.0) * jnp.cos(freq)).astype(jnp.bfloat16)
    partial_scores = lax.dot_general(
        basis.astype(jnp.bfloat16), features, (((1,), (1,)), ((), ())),
        preferred_element_type=jnp.float32,
    )
    projections = lax.psum(partial_scores, "feat") / math.sqrt(features_total)
    update_part = jnp.dot(
        projections.astype(jnp.bfloat16), features, preferred_element_type=jnp.float32
    )
    grown = basis + lax.psum(update_part, "samp") / math.sqrt(span_total)
    gram = lax.psum(jnp.dot(grown, grown.T, precision=HIGHEST), "feat")
    lower = jnp.linalg.cholesky(gram / features_total)
    return jax.scipy.linalg.solve_triangular(lower, grown, lower=True), projections


def solution(mesh):
    feats, samps = mesh.shape["feat"], mesh.shape["samp"]

    def local(embeddings, sign_bits, perms, gauss, scale, phase, basis):
        rows, width = embeddings.shape
        fits = (
            rows % BLOCK == 0
            and width % (2 * BLOCK) == 0
            and perms.shape[0] == 1
            and basis.shape[0] == 64
            and feats == 4
            and samps == 4
            and rows >= 2 * BLOCK
        )
        body = functools.partial(fused, feats, samps) if fits else general
        return body(embeddings, sign_bits, perms, gauss, scale, phase, basis)

    placed = (
        P(("grp", "samp"), None),
        P("feat"),
        P("feat", None),
        P("feat"),
        P("feat"),
        P("feat"),
        P("grp", "feat"),
    )
    return jax.shard_map(
        local,
        mesh=mesh,
        in_specs=placed,
        out_specs=(P("grp", "feat"), P("grp", "samp")),
        check_vma=False,
    )
```

```python
import functools
import math

import jax
import jax.numpy as jnp
import numpy as np
from jax import lax
from jax.experimental import pallas as pl
from jax.experimental.pallas import tpu as pltpu
from jax.sharding import PartitionSpec as P

MESH = pl.DeviceIdType.MESH
BLOCK = 256
TAIL = 128
PASSED = 2
HIGHEST = lax.Precision.HIGHEST


def cosine_coefficients(degree):
    nodes = np.cos(np.pi * (np.arange(400) + 0.5) / 400)
    squares = (nodes + 1) / 8
    fitted = np.polynomial.Chebyshev.fit(
        squares, np.cos(2 * np.pi * np.sqrt(squares)), degree, domain=[0, 0.25]
    )
    return [float(c) * math.sqrt(2.0) for c in fitted.convert(kind=np.polynomial.Polynomial).coef]


COS = cosine_coefficients(5)


def parity_sign(bits):
    for shift in (8, 4, 2, 1):
        bits = bits ^ jnp.right_shift(bits, shift)
    return (1 - 2 * (bits & 1)).astype(jnp.float32)


def scaled_cosine(turns):
    rest = turns - jnp.round(turns)
    square = rest * rest
    total = jnp.full_like(square, COS[-1])
    for c in COS[-2::-1]:
        total = total * square + c
    return total


def transform(blocks):
    stride = 1
    while stride < len(blocks):
        result = list(blocks)
        for i in range(len(blocks)):
            if not i & stride:
                result[i] = blocks[i] + blocks[i + stride]
                result[i + stride] = blocks[i] - blocks[i + stride]
        blocks = result
        stride *= 2
    return blocks


def split(x):
    high = x.astype(jnp.bfloat16)
    rest = x - high.astype(jnp.float32)
    middle = rest.astype(jnp.bfloat16)
    low = (rest - middle.astype(jnp.float32)).astype(jnp.bfloat16)
    return high, middle, low


def inverse_factor(gram):
    size = gram.shape[0]
    row = lax.broadcasted_iota(jnp.int32, (8, size), 0)
    lane = lax.broadcasted_iota(jnp.int32, (8, size), 1)
    width = 2 * size
    sub = lax.broadcasted_iota(jnp.int32, (8, width), 0)
    groups = [
        jnp.concatenate(
            [(lane == row + 8 * g).astype(jnp.float32), gram[8 * g : 8 * g + 8]], axis=1
        )
        for g in range(size // 8)
    ]
    pivots = [jnp.ones((8, width), jnp.float32) for _ in groups]
    step = 8

    def spread(x):
        return jnp.broadcast_to(x, (8, width))

    for own in range(size // 8):
        first = size + own * step
        live = range(own, size // 8)
        rows = [spread(groups[own][k : k + 1]) for k in range(step)]
        cols = [
            {g: spread(groups[g][:, first + k : first + k + 1]) for g in live}
            for k in range(step)
        ]
        cross = {
            (k, m): spread(cols[m][own][k : k + 1]) for k in range(step) for m in range(k + 1)
        }
        for k in range(step):
            if k % 2:
                inverse = ahead
            else:
                inverse = 1.0 / cross[k, k]
                minor = cross[k, k] * cross[k + 1, k + 1] - cross[k + 1, k] * cross[k + 1, k]
                ahead = cross[k, k] / minor
            pivots[own] = jnp.where(sub == k, cross[k, k], pivots[own])
            factor = {later: cross[later, k] * inverse for later in range(k + 1, step)}
            for later in range(k + 1, step):
                for m in range(k + 1, later + 1):
                    cross[later, m] = cross[later, m] - factor[later] * cross[m, k]
            for later in range(k + 1, step):
                rows[later] = rows[later] - factor[later] * rows[k]
                for g in live:
                    cols[later][g] = cols[later][g] - factor[later] * cols[k][g]
            for g in live:
                weight = cols[k][g] * inverse
                if g == own:
                    weight = jnp.where(sub > k, weight, 0.0)
                groups[g] = groups[g] - weight * rows[k]
    scaled = [g / jnp.sqrt(p) for g, p in zip(groups, pivots)]
    return jnp.concatenate(scaled, axis=0)[:, :size]


def kernel(
    feats, samps, emb_in, bits_in, perm_in, gauss_in, scale_in, phase_in, basis_in,
    proj, grown, gram_out,
    emb, bits, perm, gauss, scale, phase, basis,
    table, small, features, even, odd, scores, score_recv,
    upd, upd_recv, pair, halves, grams,
    s1, r1, s2, r2, s3, r3, s4, r4, s5, r5, r6, loads, emb_loads,
):
    me = lax.axis_index("feat")
    my = lax.axis_index("samp")
    rows, width = emb.shape
    order = basis.shape[1]
    pieces = rows // BLOCK
    share = order // feats
    cuts = [(i, 0, BLOCK) for i in range(pieces - 1)]
    cuts += [(pieces - 1, k * TAIL, TAIL) for k in range(BLOCK // TAIL)]
    half = width // 2
    core = lax.rem(my, 2)
    sibling = my + 1 - 2 * core
    partner = lax.rem(my + 2, samps)
    blocks = width // BLOCK

    def piece_rows(i):
        return slice(i * BLOCK, (i + 1) * BLOCK)

    def share_rows(owner):
        return pl.ds(pl.multiple_of(owner * share, share), share)

    def half_cols(which):
        return slice(which * half, (which + 1) * half)

    def drain(place, sem):
        pltpu.make_async_copy(place, place, sem).wait()

    emb_copies = [
        pltpu.make_async_copy(
            emb_in.at[piece_rows(i), :], emb.at[piece_rows(i), :], emb_loads.at[i]
        )
        for i in range(pieces)
    ]
    pairs = (
        (perm_in, perm, 0), (bits_in, bits, 1), (gauss_in, gauss, 2), (scale_in, scale, 3),
        (phase_in, phase, 4), (basis_in.at[:, half_cols(0)], basis.at[0], 5),
        (basis_in.at[:, half_cols(1)], basis.at[1], 5),
    )
    parameters = [
        pltpu.make_async_copy(source, place, loads.at[n]) for source, place, n in pairs
    ]
    for load in parameters[:-2]:
        load.start()
    emb_copies[0].start()
    for load in parameters[-2:]:
        load.start()
    for load in emb_copies[1:]:
        load.start()
    barrier = pltpu.get_barrier_semaphore()
    mate = me + 1 - 2 * lax.rem(me, 2)
    across = lax.rem(me + 2, feats)
    opposite = lax.rem(mate + 2, feats)
    others = [opposite, across, mate]
    for to in others:
        pl.semaphore_signal(barrier, inc=1, device_id={"feat": to}, device_id_type=MESH)
    for to in (sibling, partner):
        pl.semaphore_signal(barrier, inc=1, device_id={"samp": to}, device_id_type=MESH)

    square = (BLOCK, BLOCK)
    small[...] = parity_sign(
        lax.broadcasted_iota(jnp.int32, square, 0) & lax.broadcasted_iota(jnp.int32, square, 1)
    ).astype(jnp.bfloat16)
    parameters[0].wait()
    places = perm[...]
    base = parity_sign(lax.broadcasted_iota(jnp.int32, (128, width), 0) & places & 127).astype(
        jnp.bfloat16
    )
    for a in range(width // 128):
        flips = parity_sign(jnp.right_shift(places, 7) & a).astype(jnp.bfloat16)
        table[a * 128 : (a + 1) * 128, :] = base * flips
    for load in parameters[1:-2]:
        load.wait()
    signs = (2 * bits[...] - 1).astype(jnp.float32).astype(jnp.bfloat16)
    gains = gauss[...]
    rate = scale[...] * (1.0 / (2.0 * math.pi * width))
    offset = phase[...] * (1.0 / (2.0 * math.pi))

    def copy(src, dst, send, recv, axis, to):
        return pltpu.make_async_remote_copy(
            src_ref=src, dst_ref=dst, send_sem=send, recv_sem=recv,
            device_id={axis: to}, device_id_type=MESH,
        )

    mixes = (even, odd)

    def mix(i, n):
        cols = slice(n * BLOCK, (n + 1) * BLOCK)
        signed = emb[piece_rows(i), :] * signs
        first = jnp.dot(signed, table[:, cols], preferred_element_type=jnp.float32)
        first = first.astype(jnp.bfloat16).astype(jnp.float32)
        mixes[i % 2][:, cols] = (first * gains[:, cols]).astype(jnp.bfloat16)

    def second(i, first, size):
        mixed = mixes[i % 2]
        return transform([
            jnp.dot(
                mixed[first : first + size, n * BLOCK : (n + 1) * BLOCK], small[...],
                preferred_element_type=jnp.float32,
            )
            for n in range(blocks)
        ])

    def wave(where, n, part):
        cols = slice(n * BLOCK, (n + 1) * BLOCK)
        turns = part * rate[:, cols] + offset[:, cols]
        features[where, cols] = scaled_cosine(turns).astype(jnp.bfloat16)

    def cut_rows(cut):
        i, first, size = cut
        return slice(i * BLOCK + first, i * BLOCK + first + size)

    def cut_cols(cut):
        return slice(cut[1], cut[1] + cut[2])

    def score(cut, basis_low):
        scores[cut[0], :, cut_cols(cut)] = lax.dot_general(
            basis_low, features[cut_rows(cut), :], (((1,), (1,)), ((), ())),
            preferred_element_type=jnp.float32,
        )

    def score_copy(n, owner, source, to):
        i, cols = cuts[n][0], cut_cols(cuts[n])
        return copy(
            scores.at[i, share_rows(owner), cols], score_recv.at[i, source, :, cols],
            s1.at[0], r1.at[n], "feat", to,
        )

    emb_copies[0].wait()
    for n in range(blocks):
        mix(0, n)
    for n, cut in enumerate(cuts):
        i, first, size = cut
        if i + 1 < pieces:
            emb_copies[i + 1].wait()
        parts = second(*cut)
        for m in range(blocks):
            if i + 1 < pieces:
                mix(i + 1, m)
            wave(cut_rows(cut), m, parts[m])
        if n == 0:
            drain(basis, loads.at[5])
            basis_low = jnp.concatenate([basis[0], basis[1]], axis=1).astype(jnp.bfloat16)
        score(cut, basis_low)
        if n == 0:
            pl.semaphore_wait(barrier, feats + 1)
        for to in others:
            score_copy(n, to, me, to).start()

    def proj_copy(n, owner, to):
        place = proj.at[cuts[n][0], share_rows(owner), cut_cols(cuts[n])]
        return copy(place, place, s2.at[0], r2.at[n], "feat", to)

    def across_copy(n, owner):
        place = proj.at[cuts[n][0], share_rows(owner), cut_cols(cuts[n])]
        return copy(place, place, s2.at[0], r6.at[n], "feat", across)

    def pass_on(n):
        across_copy(n, across).wait_recv()
        proj_copy(n, across, mate).start()

    def add_all(n):
        i, cols = cuts[n][0], cut_cols(cuts[n])
        total = scores[i, share_rows(me), cols]
        drain(score_recv.at[i, 1:feats, :, cols], r1.at[n])
        for source in others:
            total = total + score_recv[i, source, :, cols]
        proj[i, share_rows(me), cols] = total * (1.0 / math.sqrt(width * feats))
        if n < PASSED:
            across_copy(n, me).start()
            proj_copy(n, me, mate).start()
            return
        for to in others:
            proj_copy(n, me, to).start()

    for n in range(len(cuts)):
        add_all(n)
    for n in range(PASSED):
        pass_on(n)

    def upd_copy(stage, k):
        rows_of = slice(k * (order // 2), (k + 1) * (order // 2))
        source = (upd.at[1 - core, rows_of], pair.at[rows_of])[stage]
        return copy(
            source, upd_recv.at[stage, rows_of], s3.at[stage], r3.at[stage, k], "samp",
            (sibling, partner)[stage],
        )

    for n, cut in enumerate(cuts):
        late = 2 if n < PASSED else 1
        drain(proj.at[cut[0], late * share : order, cut_cols(cut)], r2.at[n])
        low = proj[cut[0], :, cut_cols(cut)].astype(jnp.bfloat16)
        for q in range(2):
            term = jnp.dot(
                low, features[cut_rows(cut), half_cols(q)],
                preferred_element_type=jnp.float32,
            )
            upd[q] = upd[q] + term if n else term

    for k in range(2):
        upd_copy(0, k).start()
    for k in range(2):
        upd_copy(0, k).wait_recv()
        rows_of = slice(k * (order // 2), (k + 1) * (order // 2))
        pair[rows_of] = upd[core, rows_of] + upd_recv[0, rows_of]
        upd_copy(1, k).start()
    for k in range(2):
        upd_copy(1, k).wait_recv()
    total = pair[...] + upd_recv[1]
    block = basis[core] + total * (1.0 / math.sqrt(rows * samps))
    grown[core] = block
    gram = lax.dot_general(
        block, block, (((1,), (1,)), ((), ())), precision=HIGHEST,
        preferred_element_type=jnp.float32,
    )
    halves[0] = jnp.concatenate([gram[: order // 2], gram[order // 2 :]], axis=1)
    half_copy = copy(halves.at[0], halves.at[1], s4.at[0], r4.at[0], "samp", sibling)
    half_copy.start()

    def grown_copy(which):
        return copy(grown.at[which], grown.at[which], s4.at[1], r4.at[1], "samp", sibling)

    grown_copy(core).start()
    half_copy.wait_recv()
    grams[me] = halves[0] + halves[1]

    def gram_copy(slot, to):
        return copy(grams.at[slot], grams.at[slot], s5.at[0], r5.at[0], "feat", to)

    for to in others:
        gram_copy(me, to).start()
    grown_copy(1 - core).wait_recv()
    drain(score_recv.at[:, 1:feats], s1.at[0])
    drain(proj.at[:, share:order, :], s2.at[0])
    drain(upd_recv.at[0], s3.at[0])
    drain(upd_recv.at[1], s3.at[1])
    half_copy.wait_send()
    grown_copy(core).wait_send()
    drain(grams.at[1:feats], r5.at[0])
    packed = grams[0]
    for slot in range(1, feats):
        packed = packed + grams[slot]
    gram_out[...] = packed * (1.0 / (width * feats))
    drain(grams.at[1:feats], s5.at[0])


def finish(proj, grown, packed, out, scores_out, result, right, out_sems, score_sems):
    pieces, order, chunk = proj.shape
    parts, _, span = grown.shape
    stores = [
        pltpu.make_async_copy(
            proj.at[slot], scores_out.at[:, slot * chunk : (slot + 1) * chunk],
            score_sems.at[0],
        )
        for slot in range(pieces)
    ]
    for store in stores:
        store.start()
    for q in range(parts):
        high, middle, low = split(grown[q])
        for n, term in enumerate((high, middle, high, low, middle, high)):
            right[q, n * order : (n + 1) * order] = term
    halves = packed[...]
    gram = jnp.concatenate([halves[:, :order], halves[:, order:]], axis=0)
    inverse = inverse_factor(gram)
    high, middle, low = split(inverse)
    left = jnp.concatenate([high, high, middle, high, middle, low], axis=1)
    for q in range(parts):
        result[q] = jnp.dot(left, right[q], preferred_element_type=jnp.float32)
        store = pltpu.make_async_copy(
            result.at[q], out.at[:, q * span : (q + 1) * span], out_sems.at[0]
        )
        store.start()
    for place, sem in ((proj, score_sems.at[0]), (result, out_sems.at[0])):
        pltpu.make_async_copy(place, place, sem).wait()


def fused(feats, samps, embeddings, sign_bits, perms, gauss, scale, phase, basis):
    rows, width = embeddings.shape
    order = basis.shape[0]
    pieces, half, share = rows // BLOCK, width // 2, order // feats
    cuts = pieces - 1 + BLOCK // TAIL
    line = (1, width)
    whole = pl.BlockSpec(memory_space=pltpu.VMEM)
    far = pl.BlockSpec(memory_space=pltpu.HBM)
    f32, bf16, dma = jnp.float32, jnp.bfloat16, pltpu.SemaphoreType.DMA
    packed = (order // 2, 2 * order)
    operands = (
        embeddings, sign_bits.reshape(line), perms.reshape(line), gauss.reshape(line),
        scale.reshape(line), phase.reshape(line), basis,
    )
    near = pl.pallas_call(
        functools.partial(kernel, feats, samps),
        out_shape=(
            pltpu.VMEM((pieces, order, BLOCK), f32),
            pltpu.VMEM((2, order, half), f32),
            pltpu.VMEM(packed, f32),
        ),
        in_specs=[far] * 7,
        out_specs=(whole, whole, whole),
        scratch_shapes=[
            pltpu.VMEM((rows, width), bf16),
            pltpu.VMEM(line, jnp.int32),
            pltpu.VMEM(line, jnp.int32),
            pltpu.VMEM(line, f32),
            pltpu.VMEM(line, f32),
            pltpu.VMEM(line, f32),
            pltpu.VMEM((2, order, half), f32),
            pltpu.VMEM((width, width), bf16),
            pltpu.VMEM((BLOCK, BLOCK), bf16),
            pltpu.VMEM((rows, width), bf16),
            pltpu.VMEM((BLOCK, width), bf16),
            pltpu.VMEM((BLOCK, width), bf16),
            pltpu.VMEM((pieces, order, BLOCK), f32),
            pltpu.VMEM((pieces, feats, share, BLOCK), f32),
            pltpu.VMEM((2, order, half), f32),
            pltpu.VMEM((2, order, half), f32),
            pltpu.VMEM((order, half), f32),
            pltpu.VMEM((2,) + packed, f32),
            pltpu.VMEM((feats,) + packed, f32),
        ]
        + [dma((1,)), dma((cuts,))] * 2
        + [dma((2,)), dma((2, 2)), dma((2,)), dma((2,))]
        + [dma((1,))] * 2
        + [dma((PASSED,)), dma((6,)), dma((pieces,))],
        compiler_params=pltpu.CompilerParams(
            collective_id=0, has_side_effects=True, vmem_limit_bytes=48 << 20
        ),
        name="oja",
    )(*[pltpu.with_memory_space_constraint(x, pltpu.HBM) for x in operands])
    near = [pltpu.with_memory_space_constraint(x, pltpu.VMEM) for x in near]
    return pl.pallas_call(
        finish,
        out_shape=(
            jax.ShapeDtypeStruct((order, width), f32),
            jax.ShapeDtypeStruct((order, rows), f32),
        ),
        in_specs=[whole] * 3,
        out_specs=(far, far),
        scratch_shapes=[
            pltpu.VMEM((2, order, half), f32),
            pltpu.VMEM((2, 6 * order, half), bf16),
            dma((1,)), dma((1,)),
        ],
        compiler_params=pltpu.CompilerParams(vmem_limit_bytes=16 << 20),
        name="finish",
    )(*near)


def sylvester(width):
    indices = lax.iota(jnp.int32, width)
    return parity_sign(indices[:, None] & indices[None, :]).astype(jnp.bfloat16)


def general(embeddings, sign_bits, perms, gauss, scale, phase, basis):
    rows, width = embeddings.shape
    table = sylvester(width)
    features_total = width * lax.axis_size("feat")
    span_total = rows * lax.axis_size("samp")
    signs = (2 * sign_bits - 1).astype(jnp.bfloat16)
    columns = parity_sign(lax.iota(jnp.int32, width)[:, None] & perms[0][None, :]).astype(
        jnp.bfloat16
    )
    first = jnp.dot(embeddings * signs, columns, preferred_element_type=jnp.float32)
    mixed = (first.astype(jnp.bfloat16) * gauss).astype(jnp.bfloat16)
    freq = jnp.dot(mixed, table, preferred_element_type=jnp.float32) * scale / width + phase
    features = (math.sqrt(2.0) * jnp.cos(freq)).astype(jnp.bfloat16)
    partial_scores = lax.dot_general(
        basis.astype(jnp.bfloat16), features, (((1,), (1,)), ((), ())),
        preferred_element_type=jnp.float32,
    )
    projections = lax.psum(partial_scores, "feat") / math.sqrt(features_total)
    update_part = jnp.dot(
        projections.astype(jnp.bfloat16), features, preferred_element_type=jnp.float32
    )
    grown = basis + lax.psum(update_part, "samp") / math.sqrt(span_total)
    gram = lax.psum(jnp.dot(grown, grown.T, precision=HIGHEST), "feat")
    lower = jnp.linalg.cholesky(gram / features_total)
    return jax.scipy.linalg.solve_triangular(lower, grown, lower=True), projections


def solution(mesh):
    feats, samps = mesh.shape["feat"], mesh.shape["samp"]

    def local(embeddings, sign_bits, perms, gauss, scale, phase, basis):
        rows, width = embeddings.shape
        fits = (
            rows % BLOCK == 0
            and width % (2 * BLOCK) == 0
            and perms.shape[0] == 1
            and basis.shape[0] == 64
            and feats == 4
            and samps == 4
            and rows >= 2 * BLOCK
        )
        body = functools.partial(fused, feats, samps) if fits else general
        return body(embeddings, sign_bits, perms, gauss, scale, phase, basis)

    placed = (
        P(("grp", "samp"), None),
        P("feat"),
        P("feat", None),
        P("feat"),
        P("feat"),
        P("feat"),
        P("grp", "feat"),
    )
    return jax.shard_map(
        local,
        mesh=mesh,
        in_specs=placed,
        out_specs=(P("grp", "feat"), P("grp", "samp")),
        check_vma=False,
    )
```
